32 devices in a mesh: shard: 4 (over y, core), replica: 8 (over z, x).
Axes of the slice: x: 2, y: 2, z: 4, core: 2. Of those that a mesh axis runs over, the one named last changes fastest.
Arguments:
- tokens: bfloat16 [32, 512, 1024], P(('shard', 'replica')), may hold values from -10 to 10
- cotangent: bfloat16 [32, 512, 1024], P(('shard', 'replica')), may hold values from -6 to 6
- w_query: bfloat16 [1024, 1024], P('shard'), may hold values from -1 to 1
- w_key: bfloat16 [1024, 1024], P('shard'), may hold values from -1 to 1
- w_value: bfloat16 [1024, 1024], P('shard'), may hold values from -0.1875 to 0.1875
- w_output: bfloat16 [1024, 1024], P('shard'), may hold values from -0.1875 to 0.1875
- w_gate: bfloat16 [1024, 4096], P('shard'), may hold values from -0.1875 to 0.1875
- w_up: bfloat16 [1024, 4096], P('shard'), may hold values from -0.1875 to 0.1875
- w_down: bfloat16 [4096, 1024], P('shard'), may hold values from -0.09375 to 0.09375
- query_gain: bfloat16 [1024], P('shard'), may hold values from 0.5 to 1.5
- key_gain: bfloat16 [1024], P('shard'), may hold values from 0.5 to 1.5
- attn_gain: bfloat16 [1024], P('shard'), may hold values from 0.5 to 1.5
- mlp_gain: bfloat16 [1024], P('shard'), may hold values from 0.5 to 1.5
Outputs:
- block_out: bfloat16 [32, 512, 1024], P(('shard', 'replica'))
- grad_tokens: float32 [32, 512, 1024], P(('shard', 'replica'))
- grad_w_query: float32 [1024, 1024], P('shard')
- grad_w_key: float32 [1024, 1024], P('shard')
- grad_w_value: float32 [1024, 1024], P('shard')
- grad_w_output: float32 [1024, 1024], P('shard')
- grad_w_gate: float32 [1024, 4096], P('shard')
- grad_w_up: float32 [1024, 4096], P('shard')
- grad_w_down: float32 [4096, 1024], P('shard')
- grad_query_gain: float32 [1024], P('shard')
- grad_key_gain: float32 [1024], P('shard')
- grad_attn_gain: float32 [1024], P('shard')
- grad_mlp_gain: float32 [1024], P('shard')
The draws below stay inside these ranges and needn't reach their ends.
All inputs are finite; a program needn't handle non-finite values.
Results may differ from the reference program's by a relative error of at most 0.022.
Values may be sent and summed in bfloat16 or wider, within the bound.
No kernel may reach another device: no remote copies, remote signals or barrier semaphores. Data moves between devices by JAX's collectives and lax.ppermute only.
A program may use at most 256 MiB of HBM per device.

```python
import jax
import jax.numpy as jnp
from jax import lax

D = 1024
HEADS = 8
HD = 128
FF = 4096
LEN = 512
HQ = 1024
SEQS = 32


def drawn_weight(key, salt):
    return jax.random.truncated_normal(jax.random.fold_in(key, salt), -6.0, 6.0, (D, HQ), jnp.float32) * D ** (-0.5)


def drawn_gain(key, salt):
    return jax.random.uniform(jax.random.fold_in(key, salt), (HQ,), jnp.float32, 0.5, 1.5)


def draw_w_query(key, part):
    normal_part = drawn_weight(key, 31)
    return normal_part.astype(jnp.bfloat16)


def draw_w_key(key, part):
    normal_part = drawn_weight(key, 37)
    return normal_part.astype(jnp.bfloat16)


def draw_query_gain(key, part):
    gain_part = drawn_gain(key, 41)
    return gain_part.astype(jnp.bfloat16)


def draw_key_gain(key, part):
    gain_part = drawn_gain(key, 47)
    return gain_part.astype(jnp.bfloat16)


def draw_tokens(key, part):
    normal_part = jax.random.truncated_normal(jax.random.fold_in(key, 21), -6.0, 6.0, (SEQS, LEN, D), jnp.float32)
    return normal_part.astype(jnp.bfloat16)


def block_scale(stream_key, extent, cuts, smallest, high):
    loudness, own = 1.0, jax.random.fold_in(stream_key, 6)
    for axis_at, blocks in cuts:
        draws = jnp.exp(jax.random.uniform(jax.random.fold_in(own, axis_at), (blocks,), jnp.float32, smallest / len(cuts), high / len(cuts)))
        loudness = loudness * jnp.repeat(draws, extent[axis_at] // blocks).reshape([-1 if axis == axis_at else 1 for axis in range(len(extent))])
    return loudness


def noise(rng, dims, spread, most, cuts=(), held_as=jnp.bfloat16):
    drawn = spread * jax.random.normal(rng, dims, jnp.float32)
    if cuts:
        drawn = drawn * block_scale(rng, dims, cuts, -0.22, 0.18)
    return jnp.clip(drawn, -most, most).astype(held_as)


def setup_inputs(seed: int = 0) -> dict:
    keys = jax.random.split(jax.random.key(seed), 14)
    return {
        "tokens": draw_tokens(jax.random.fold_in(keys[13], 71), 0),
        "cotangent": noise(keys[1], (SEQS, LEN, D), 1.0, 6.0, ((0, 32),)),
        "w_query": draw_w_query(jax.random.fold_in(keys[13], 71), 0),
        "w_key": draw_w_key(jax.random.fold_in(keys[13], 71), 0),
        "w_value": noise(keys[4], (D, HQ), D ** -0.5, 0.1875, ((0, 4),)),
        "w_output": noise(keys[5], (HQ, D), HQ ** -0.5, 0.1875, ((0, 4),)),
        "w_gate": noise(keys[6], (D, FF), D ** -0.5, 0.1875, ((0, 4),)),
        "w_up": noise(keys[7], (D, FF), D ** -0.5, 0.1875, ((0, 4),)),
        "w_down": noise(keys[8], (FF, D), FF ** -0.5, 0.09375, ((0, 4),)),
        "query_gain": draw_query_gain(jax.random.fold_in(keys[13], 71), 0),
        "key_gain": draw_key_gain(jax.random.fold_in(keys[13], 71), 0),
        "attn_gain": jnp.clip(0.5 + 1.0 * jax.random.uniform(keys[11], (D,), jnp.float32) ** block_scale(keys[11], (D,), ((0, 4),), -0.2, 0.2), 0.5, 1.5).astype(jnp.bfloat16),
        "mlp_gain": jnp.clip(0.5 + 1.0 * jax.random.uniform(keys[12], (D,), jnp.float32) ** block_scale(keys[12], (D,), ((0, 4),), -0.2, 0.2), 0.5, 1.5).astype(jnp.bfloat16),
    }


EPS = 1e-06
THETA = 500000.0

def rms_scale(values):
    return lax.rsqrt(lax.optimization_barrier(jnp.mean(values * values, axis=-1, keepdims=True)) + EPS)

def norm_back(gradient, values, scale, gain):
    scaled = gradient * gain
    return scale * (scaled - values * scale * scale * lax.optimization_barrier(jnp.mean(scaled * values, axis=-1, keepdims=True)))

def rope_tables(length, head_size):
    half_size = head_size // 2
    frequency = THETA ** (-2.0 * jnp.arange(half_size, dtype=jnp.float32) / head_size)
    angles = jnp.arange(length, dtype=jnp.float32)[:, None] * frequency[None, :]
    return (jnp.cos(angles), jnp.sin(angles))

def rotate(values, cosine, sine_table):
    half_size = values.shape[-1] // 2
    first_half = values[..., :half_size]
    second_half = values[..., half_size:]
    cos_wide = cosine[:, None, :]
    sin_wide = sine_table[:, None, :]
    return jnp.concatenate([first_half * cos_wide - second_half * sin_wide, second_half * cos_wide + first_half * sin_wide], axis=-1)

def block_pass(tokens, cotangent, w_query, w_key, w_value, w_output, w_gate, w_up, w_down, query_gain, key_gain, attn_gain, mlp_gain):
    seq_count, length, model_width = tokens.shape
    row_count = seq_count * length
    token_rows = tokens.reshape(row_count, model_width)
    cosine, sine_table = rope_tables(length, HD)
    positions = jnp.arange(length)
    causal = positions[:, None] >= positions[None, :]
    factor = HD ** (-0.5)
    gain_query = query_gain.astype(jnp.float32)
    gain_key = key_gain.astype(jnp.float32)
    gain_attn = attn_gain.astype(jnp.float32)
    gain_mlp = mlp_gain.astype(jnp.float32)
    query_raw = jnp.dot(token_rows, w_query, preferred_element_type=jnp.float32)
    key_raw = jnp.dot(token_rows, w_key, preferred_element_type=jnp.float32)
    value_raw = jnp.dot(token_rows, w_value, preferred_element_type=jnp.float32)
    query_scale = rms_scale(query_raw)
    key_scale = rms_scale(key_raw)
    query_rot = rotate((query_raw * query_scale * gain_query).reshape(seq_count, length, HEADS, HD), cosine, sine_table).astype(jnp.bfloat16)
    key_rot = rotate((key_raw * key_scale * gain_key).reshape(seq_count, length, HEADS, HD), cosine, sine_table).astype(jnp.bfloat16)
    value_heads = value_raw.astype(jnp.bfloat16).reshape(seq_count, length, HEADS, HD)
    scores = jnp.einsum('blhd,bmhd->bhlm', query_rot.astype(jnp.float32), key_rot.astype(jnp.float32)) * factor
    scores = jnp.where(causal, scores, -jnp.inf)
    row_max = lax.optimization_barrier(jnp.max(scores, axis=-1, keepdims=True))
    log_total = row_max + jnp.log(lax.optimization_barrier(jnp.sum(jnp.exp(scores - row_max), axis=-1, keepdims=True)))
    attn_probs = jnp.exp(scores - log_total)
    attn_rounded = attn_probs.astype(jnp.bfloat16)
    mixed = jnp.einsum('bhlm,bmhd->blhd', attn_rounded.astype(jnp.float32), value_heads.astype(jnp.float32))
    mixed = mixed.astype(jnp.bfloat16).reshape(row_count, HEADS * HD)
    attn_out = jnp.dot(mixed, w_output, preferred_element_type=jnp.float32)
    attn_scale = rms_scale(attn_out)
    hidden_res = token_rows.astype(jnp.float32) + attn_out * attn_scale * gain_attn
    hidden_bf = hidden_res.astype(jnp.bfloat16)
    gate_raw = jnp.dot(hidden_bf, w_gate, preferred_element_type=jnp.float32)
    up_raw = jnp.dot(hidden_bf, w_up, preferred_element_type=jnp.float32)
    gate_sig = jax.nn.sigmoid(gate_raw)
    product = (gate_raw * gate_sig * up_raw).astype(jnp.bfloat16)
    ffn_out = jnp.dot(product, w_down, preferred_element_type=jnp.float32)
    ffn_scale = rms_scale(ffn_out)
    block_out = (hidden_res + ffn_out * ffn_scale * gain_mlp).astype(jnp.bfloat16)
    grad_out = cotangent.reshape(row_count, model_width).astype(jnp.float32)
    grad_mlp_gain = lax.optimization_barrier(jnp.sum(grad_out * ffn_out * ffn_scale, axis=0))
    grad_ffn = norm_back(grad_out, ffn_out, ffn_scale, gain_mlp).astype(jnp.bfloat16)
    grad_down = jnp.dot(product.T, grad_ffn, preferred_element_type=jnp.float32)
    grad_product = jnp.dot(grad_ffn, w_down.T, preferred_element_type=jnp.float32)
    grad_up_in = (grad_product * gate_raw * gate_sig).astype(jnp.bfloat16)
    grad_gate_in = (grad_product * up_raw * gate_sig * (1.0 + gate_raw * (1.0 - gate_sig))).astype(jnp.bfloat16)
    grad_gate = jnp.dot(hidden_bf.T, grad_gate_in, preferred_element_type=jnp.float32)
    grad_up = jnp.dot(hidden_bf.T, grad_up_in, preferred_element_type=jnp.float32)
    grad_hidden = grad_out + jnp.dot(grad_gate_in, w_gate.T, preferred_element_type=jnp.float32) + jnp.dot(grad_up_in, w_up.T, preferred_element_type=jnp.float32)
    grad_attn_gain = lax.optimization_barrier(jnp.sum(grad_hidden * attn_out * attn_scale, axis=0))
    grad_attn = norm_back(grad_hidden, attn_out, attn_scale, gain_attn).astype(jnp.bfloat16)
    grad_output = jnp.dot(mixed.T, grad_attn, preferred_element_type=jnp.float32)
    grad_mixed = jnp.dot(grad_attn, w_output.T, preferred_element_type=jnp.float32).astype(jnp.bfloat16)
    grad_mixed = grad_mixed.reshape(seq_count, length, HEADS, HD)
    grad_value_in = jnp.einsum('bhlm,blhd->bmhd', attn_rounded.astype(jnp.float32), grad_mixed.astype(jnp.float32))
    grad_value_in = grad_value_in.astype(jnp.bfloat16).reshape(row_count, HEADS * HD)
    grad_probs = jnp.einsum('blhd,bmhd->bhlm', grad_mixed.astype(jnp.float32), value_heads.astype(jnp.float32))
    row_dot = lax.optimization_barrier(jnp.sum(attn_probs * grad_probs, axis=-1, keepdims=True))
    grad_scores = (attn_probs * (grad_probs - row_dot) * factor).astype(jnp.bfloat16)
    grad_query_rot = jnp.einsum('bhlm,bmhd->blhd', grad_scores.astype(jnp.float32), key_rot.astype(jnp.float32))
    grad_key_rot = jnp.einsum('bhlm,blhd->bmhd', grad_scores.astype(jnp.float32), query_rot.astype(jnp.float32))
    grad_query_norm = rotate(grad_query_rot, cosine, -sine_table).reshape(row_count, HEADS * HD)
    grad_key_norm = rotate(grad_key_rot, cosine, -sine_table).reshape(row_count, HEADS * HD)
    grad_query_gain = lax.optimization_barrier(jnp.sum(grad_query_norm * query_raw * query_scale, axis=0))
    grad_key_gain = lax.optimization_barrier(jnp.sum(grad_key_norm * key_raw * key_scale, axis=0))
    grad_query_in = norm_back(grad_query_norm, query_raw, query_scale, gain_query).astype(jnp.bfloat16)
    grad_key_in = norm_back(grad_key_norm, key_raw, key_scale, gain_key).astype(jnp.bfloat16)
    grad_wq = jnp.dot(token_rows.T, grad_query_in, preferred_element_type=jnp.float32)
    grad_wk = jnp.dot(token_rows.T, grad_key_in, preferred_element_type=jnp.float32)
    grad_wv = jnp.dot(token_rows.T, grad_value_in, preferred_element_type=jnp.float32)
    grad_tokens = grad_hidden + jnp.dot(grad_query_in, w_query.T, preferred_element_type=jnp.float32)
    grad_tokens = grad_tokens + jnp.dot(grad_key_in, w_key.T, preferred_element_type=jnp.float32)
    grad_tokens = grad_tokens + jnp.dot(grad_value_in, w_value.T, preferred_element_type=jnp.float32)
    gradients = (grad_wq, grad_wk, grad_wv, grad_output, grad_gate, grad_up, grad_down, grad_query_gain, grad_key_gain, grad_attn_gain, grad_mlp_gain)
    return (block_out.reshape(seq_count, length, model_width), grad_tokens.reshape(seq_count, length, model_width), gradients)

def reference(tokens, cotangent, w_query, w_key, w_value, w_output, w_gate, w_up, w_down, query_gain, key_gain, attn_gain, mlp_gain):
    seqs_all = tokens.shape[0]
    seq_length = tokens.shape[1]
    model_width = tokens.shape[2]
    group_size = 8 if seqs_all % 8 == 0 else 1
    block_count = seqs_all // group_size
    token_blocks = tokens.reshape(block_count, group_size, seq_length, model_width)
    cot_blocks = cotangent.reshape(block_count, group_size, seq_length, model_width)
    weights = (w_query, w_key, w_value, w_output, w_gate, w_up, w_down, query_gain, key_gain, attn_gain, mlp_gain)

    def step(totals, pieces):
        block_out, grad_rows, gradients = block_pass(pieces[0], pieces[1], *weights)
        updated = tuple((total + extra for total, extra in zip(totals, gradients)))
        return (updated, (block_out, grad_rows))
    zeros_init = tuple((jnp.zeros(weight.shape, jnp.float32) for weight in weights))
    totals, outputs = lax.scan(step, zeros_init, (token_blocks, cot_blocks))
    factor = float(seqs_all * seq_length) ** (-0.5)
    return (outputs[0].reshape(seqs_all, seq_length, model_width), outputs[1].reshape(seqs_all, seq_length, model_width), totals[0] * factor, totals[1] * factor, totals[2] * factor, totals[3] * factor, totals[4] * factor, totals[5] * factor, totals[6] * factor, totals[7] * factor, totals[8] * factor, totals[9] * factor, totals[10] * factor)
```

```python
import jax
import jax.numpy as jnp
from jax import lax
from jax.sharding import PartitionSpec as P

HD = 128


EPS = 1e-06
THETA = 500000.0


def rms_scale(values):
    return lax.rsqrt(jnp.mean(values * values, axis=-1, keepdims=True) + EPS)


def norm_back(gradient, values, scale, gain):
    scaled = gradient * gain
    return scale * (
        scaled - values * scale * scale * jnp.mean(scaled * values, axis=-1, keepdims=True)
    )


def rope_tables(length, head_size):
    half_size = head_size // 2
    frequency = THETA ** (-2.0 * jnp.arange(half_size, dtype=jnp.float32) / head_size)
    angles = jnp.arange(length, dtype=jnp.float32)[:, None] * frequency[None, :]
    return (jnp.cos(angles), jnp.sin(angles))


def rotate(values, cosine, sine_table):
    half_size = values.shape[-1] // 2
    first_half = values[..., :half_size]
    second_half = values[..., half_size:]
    cos_wide = cosine[:, None, :]
    sin_wide = sine_table[:, None, :]
    return jnp.concatenate(
        [
            first_half * cos_wide - second_half * sin_wide,
            second_half * cos_wide + first_half * sin_wide,
        ],
        axis=-1,
    )


def project(rows, weight):
    return jnp.dot(rows, weight, preferred_element_type=jnp.float32)


def back_project(rows, weight):
    return jnp.einsum("tf,df->td", rows, weight, preferred_element_type=jnp.float32)


def outer_sum(left, right):
    return jnp.einsum("td,tf->df", left, right, preferred_element_type=jnp.float32)


def pairs(axis, bit):
    return [(i, i ^ bit) for i in range(lax.axis_size(axis))]


def swap(value, axis, bit):
    return lax.ppermute(value, axis, pairs(axis, bit))


def bit_of(axis, bit):
    return jnp.where((lax.axis_index(axis) & bit) != 0, 1, 0)


def part_of(value, index, count):
    size = value.shape[0] // count
    return lax.dynamic_slice_in_dim(value, index * size, size, 0)


def ordered(first_is_mine, mine, other):
    return jnp.where(
        first_is_mine, jnp.concatenate([mine, other], 0), jnp.concatenate([other, mine], 0)
    )


def bits_below(size):
    out, bit = [], 1
    while bit < size:
        out.append(bit)
        bit *= 2
    return out


def gather_pieces(shard_rows, order):
    near = swap(shard_rows, "shard", 1)
    bits = bits_below(lax.axis_size("replica"))[:2]
    if order:
        bits = bits[::-1]
    count = 2 ** len(bits)
    index = 0
    for bit in bits:
        index = index * 2 + bit_of("replica", bit)
    held = swap(part_of(shard_rows, index, count), "shard", 2)
    for bit in bits[::-1]:
        other = swap(held, "replica", bit)
        held = ordered(bit_of("replica", bit) == 0, held, other)
    far = held
    both = swap(far, "shard", 1)
    return (shard_rows, near, far, both)


def assemble(pieces):
    me = lax.axis_index("shard")
    rows = pieces[0].shape[0]
    full = jnp.zeros((4 * rows,) + pieces[0].shape[1:], pieces[0].dtype)
    for step, piece in enumerate(pieces):
        full = lax.dynamic_update_slice_in_dim(full, piece, (me ^ step) * rows, 0)
    return full


def block(value, index, count):
    size = value.shape[1] // count
    return lax.dynamic_slice_in_dim(value, index * size, size, 1)


def reduce_rows(left, right, scale):
    me = lax.axis_index("shard")
    groups = lax.axis_size("shard")

    def term(which):
        return outer_sum(block(left, which, groups), right)

    sent = jnp.concatenate(
        [term(me ^ 3).astype(jnp.bfloat16), term(me ^ 1).astype(jnp.bfloat16)], 0
    )
    got = swap(sent, "shard", 1)
    half = got.shape[0] // 2
    away = (term(me ^ 2) + got[:half].astype(jnp.float32)).astype(jnp.bfloat16)
    back = swap(away, "shard", 2)
    held = (
        term(me) + got[half:].astype(jnp.float32) + back.astype(jnp.float32)
    ).astype(jnp.bfloat16)
    bits = bits_below(lax.axis_size("replica"))
    for bit in bits:
        at = bit_of("replica", bit)
        other = swap(part_of(held, 1 - at, 2), "replica", bit)
        held = part_of(held, at, 2) + other
    for bit in bits[::-1]:
        other = swap(held, "replica", bit)
        held = ordered(bit_of("replica", bit) == 0, held, other)
    return held.astype(jnp.float32) * scale


def sum_all(value):
    for axis in ("shard", "replica"):
        for bit in bits_below(lax.axis_size(axis)):
            value = value + swap(value, axis, bit)
    return value


def local(
    tokens,
    cotangent,
    w_query,
    w_key,
    w_value,
    w_output,
    w_gate,
    w_up,
    w_down,
    query_gain,
    key_gain,
    attn_gain,
    mlp_gain,
):
    seq_count, length, model_width = tokens.shape
    row_count = seq_count * length
    token_rows = tokens.reshape(row_count, model_width)
    grad_factor = float(lax.axis_size("shard") * lax.axis_size("replica") * row_count) ** (-0.5)
    cosine, sine_table = rope_tables(length, HD)
    causal = lax.broadcasted_iota(jnp.int32, (length, length), 0) >= lax.broadcasted_iota(
        jnp.int32, (length, length), 1
    )
    factor = HD ** (-0.5)
    gains = jnp.stack([query_gain, key_gain, attn_gain, mlp_gain]).astype(jnp.float32)
    gains = jnp.concatenate([gains, gains], 0)
    gains = assemble(
        (
            gains.T,
            swap(gains.T, "shard", 1),
            swap(gains.T, "shard", 2),
            swap(swap(gains.T, "shard", 1), "shard", 2),
        )
    )
    gain_query, gain_key, gain_attn, gain_mlp = gains.T[:4]
    full_query = assemble(gather_pieces(w_query, 0))
    full_key = assemble(gather_pieces(w_key, 1))
    full_value = assemble(gather_pieces(w_value, 0))
    full_output = assemble(gather_pieces(w_output, 1))
    full_gate = assemble(gather_pieces(w_gate, 0))
    full_up = assemble(gather_pieces(w_up, 1))
    full_down = assemble(gather_pieces(w_down, 0))
    head_count = full_query.shape[1] // HD
    query_raw = project(token_rows, full_query)
    key_raw = project(token_rows, full_key)
    value_raw = project(token_rows, full_value)
    query_scale = rms_scale(query_raw)
    key_scale = rms_scale(key_raw)
    query_rot = rotate(
        (query_raw * query_scale * gain_query).reshape(seq_count, length, head_count, HD),
        cosine,
        sine_table,
    ).astype(jnp.bfloat16)
    key_rot = rotate(
        (key_raw * key_scale * gain_key).reshape(seq_count, length, head_count, HD),
        cosine,
        sine_table,
    ).astype(jnp.bfloat16)
    value_heads = value_raw.astype(jnp.bfloat16).reshape(seq_count, length, head_count, HD)
    scores = (
        jnp.einsum("blhd,bmhd->bhlm", query_rot, key_rot, preferred_element_type=jnp.float32)
        * factor
    )
    scores = jnp.where(causal, scores, -jnp.inf)
    row_max = jnp.max(scores, axis=-1, keepdims=True)
    log_total = row_max + jnp.log(jnp.sum(jnp.exp(scores - row_max), axis=-1, keepdims=True))
    attn_rounded = jnp.exp(scores - log_total).astype(jnp.bfloat16)
    mixed = jnp.einsum(
        "bhlm,bmhd->blhd", attn_rounded, value_heads, preferred_element_type=jnp.float32
    )
    mixed = mixed.astype(jnp.bfloat16).reshape(row_count, head_count * HD)
    attn_out = project(mixed, full_output)
    attn_scale = rms_scale(attn_out)
    hidden_res = token_rows.astype(jnp.float32) + attn_out * attn_scale * gain_attn
    hidden_bf = hidden_res.astype(jnp.bfloat16)
    gate_raw = project(hidden_bf, full_gate)
    up_raw = project(hidden_bf, full_up)
    gate_sig = jax.nn.sigmoid(gate_raw)
    product = (gate_raw * gate_sig * up_raw).astype(jnp.bfloat16)
    ffn_out = project(product, full_down)
    ffn_scale = rms_scale(ffn_out)
    block_out = (hidden_res + ffn_out * ffn_scale * gain_mlp).astype(jnp.bfloat16)
    grad_out = cotangent.reshape(row_count, model_width).astype(jnp.float32)
    grad_mlp_gain = jnp.sum(grad_out * ffn_out * ffn_scale, axis=0)
    grad_ffn = norm_back(grad_out, ffn_out, ffn_scale, gain_mlp).astype(
        jnp.bfloat16
    )
    grad_down = reduce_rows(product, grad_ffn, grad_factor)
    grad_product = back_project(grad_ffn, full_down)
    grad_up_in = (grad_product * gate_raw * gate_sig).astype(jnp.bfloat16)
    grad_gate_in = (grad_product * up_raw * gate_sig * (1.0 + gate_raw * (1.0 - gate_sig))).astype(
        jnp.bfloat16
    )
    grad_gate = reduce_rows(hidden_bf, grad_gate_in, grad_factor)
    grad_up = reduce_rows(hidden_bf, grad_up_in, grad_factor)
    grad_hidden = (
        grad_out + back_project(grad_gate_in, full_gate) + back_project(grad_up_in, full_up)
    )
    grad_attn_gain = jnp.sum(grad_hidden * attn_out * attn_scale, axis=0)
    grad_attn = norm_back(grad_hidden, attn_out, attn_scale, gain_attn).astype(
        jnp.bfloat16
    )
    grad_output = reduce_rows(mixed, grad_attn, grad_factor)
    grad_mixed = (
        back_project(grad_attn, full_output)
        .astype(jnp.bfloat16)
        .reshape(seq_count, length, head_count, HD)
    )
    scores_again = (
        jnp.einsum("blhd,bmhd->bhlm", query_rot, key_rot, preferred_element_type=jnp.float32)
        * factor
    )
    attn_probs = jnp.exp(jnp.where(causal, scores_again, -jnp.inf) - log_total)
    probs_rounded = attn_probs.astype(jnp.bfloat16)
    grad_value_in = jnp.einsum(
        "bhlm,blhd->bmhd", probs_rounded, grad_mixed, preferred_element_type=jnp.float32
    )
    grad_value_in = grad_value_in.astype(jnp.bfloat16).reshape(row_count, head_count * HD)
    grad_probs = jnp.einsum(
        "blhd,bmhd->bhlm", grad_mixed, value_heads, preferred_element_type=jnp.float32
    )
    row_dot = jnp.sum(attn_probs * grad_probs, axis=-1, keepdims=True)
    grad_scores = (attn_probs * (grad_probs - row_dot) * factor).astype(jnp.bfloat16)
    grad_query_rot = jnp.einsum(
        "bhlm,bmhd->blhd", grad_scores, key_rot, preferred_element_type=jnp.float32
    )
    grad_key_rot = jnp.einsum(
        "bhlm,blhd->bmhd", grad_scores, query_rot, preferred_element_type=jnp.float32
    )
    grad_query_norm = rotate(grad_query_rot, cosine, -sine_table).reshape(
        row_count, head_count * HD
    )
    grad_key_norm = rotate(grad_key_rot, cosine, -sine_table).reshape(row_count, head_count * HD)
    grad_query_gain = jnp.sum(grad_query_norm * query_raw * query_scale, axis=0)
    grad_key_gain = jnp.sum(grad_key_norm * key_raw * key_scale, axis=0)
    grad_query_in = norm_back(
        grad_query_norm, query_raw, query_scale, gain_query
    ).astype(jnp.bfloat16)
    grad_key_in = norm_back(grad_key_norm, key_raw, key_scale, gain_key).astype(
        jnp.bfloat16
    )
    grad_wq = reduce_rows(token_rows, grad_query_in, grad_factor)
    grad_wk = reduce_rows(token_rows, grad_key_in, grad_factor)
    grad_wv = reduce_rows(token_rows, grad_value_in, grad_factor)
    grad_tokens = (
        grad_hidden
        + back_project(grad_query_in, full_query)
        + back_project(grad_key_in, full_key)
        + back_project(grad_value_in, full_value)
    )
    gain_sums = jnp.stack([grad_query_gain, grad_key_gain, grad_attn_gain, grad_mlp_gain])
    gain_sums = sum_all(gain_sums.reshape(4, lax.axis_size("shard"), -1)) * grad_factor
    gain_sums = lax.dynamic_index_in_dim(gain_sums, lax.axis_index("shard"), 1, keepdims=False)
    return (
        block_out.reshape(seq_count, length, model_width),
        grad_tokens.reshape(seq_count, length, model_width),
        grad_wq,
        grad_wk,
        grad_wv,
        grad_output,
        grad_gate,
        grad_up,
        grad_down,
        gain_sums[0],
        gain_sums[1],
        gain_sums[2],
        gain_sums[3],
    )


def solution(mesh):
    placed = (
        P(("shard", "replica"), None, None),
        P(("shard", "replica"), None, None),
        P("shard", None),
        P("shard", None),
        P("shard", None),
        P("shard", None),
        P("shard", None),
        P("shard", None),
        P("shard", None),
        P("shard"),
        P("shard"),
        P("shard"),
        P("shard"),
    )
    return jax.shard_map(
        local,
        mesh=mesh,
        in_specs=placed,
        out_specs=(
            P(("shard", "replica"), None, None),
            P(("shard", "replica"), None, None),
            P("shard", None),
            P("shard", None),
            P("shard", None),
            P("shard", None),
            P("shard", None),
            P("shard", None),
            P("shard", None),
            P("shard"),
            P("shard"),
            P("shard"),
            P("shard"),
        ),
        check_vma=False,
    )
```
